32 devices in a mesh: clusters: 32 (over z, y, x, core).
Axes of the slice: x: 2, y: 2, z: 4, core: 2. Of those that a mesh axis runs over, the one named last changes fastest.
Arguments:
- charges: bfloat16 [8, 131072], P(None, 'clusters'), may hold values from -6 to 6
- leaf_basis: bfloat16 [32, 131072], P(None, 'clusters'), may hold values from -0.75 to 0.75
- leaf_transfer: bfloat16 [256, 64, 256], P('clusters'), may hold values from -0.375 to 0.375
- mid_transfer: bfloat16 [32, 64, 512], P('clusters'), may hold values from -0.25 to 0.25
- far_source: int32 [2048, 16], P('clusters'), may hold values from 0 to 2047, as said below
- far_coupling: bfloat16 [2048, 32, 512], P('clusters'), may hold values from -0.25 to 0.25
- mid_source: int32 [256, 8], P('clusters'), may hold values from 0 to 255, as said below
- mid_coupling: bfloat16 [256, 64, 512], P('clusters'), may hold values from -0.25 to 0.25
- box_coupling: bfloat16 [32, 64, 192], P('clusters'), may hold values from -0.4375 to 0.4375
- top_transfer: bfloat16 [28, 64, 128], replicated, may hold values from -0.5 to 0.5
- top_coupling: bfloat16 [28, 64, 192], replicated, may hold values from -0.4375 to 0.4375
- near_target: int32 [32768], P('clusters'), may hold values from 0 to 63
- near_source: int32 [32768], P('clusters'), may hold values from 0 to 2047, as said below
- near_count: int32 [32], P('clusters'), may hold values from 256 to 1024, as said below
- near_blocks: bfloat16 [64, 2097152], P(None, 'clusters'), may hold values from -0.25 to 0.25
Outputs:
- potentials: bfloat16 [8, 131072], P(None, 'clusters')
The draws below stay inside these ranges and needn't reach their ends.
Inputs may be any that keep to these rules, and one draw needn't show every extreme that they name: `far_source`: each source leaf lies in the row's box or in a box whose index differs by one; for each box and each box beside it, the far lists of the box's leaves name exactly 4 distinct leaves of the box beside it. `mid_source`: each source cluster lies in the row's box or in a box whose index differs by one. `near_source`: each source leaf lies in the slot's box or in a box whose index differs by one. `near_count`: slots at or after a box's count are not used.
All inputs are finite; a program needn't handle non-finite values.
Results may differ from the reference program's by a relative error of at most 0.0053.
Values may be sent and summed in bfloat16 or wider, within the bound.
A program may use at most 128 MiB of HBM per device.

```python
import jax
import jax.numpy as jnp
from jax import lax

M = 64
NV = 8
R0 = 32
R = 64
CHILD = 8
K0 = 16
K1 = 8
SLOT = 4
NB_CAP = 1024
BOXES = 32
LEAF_DEV = 64
NL = 2048
NL1 = 256
POINTS = 131072
NBALL = 32768
LEVELS_TOP = 3
TOPS = 28


def shuffled(subkey, length):
    return jax.random.permutation(subkey, length).astype(jnp.int32)


def draw_far_source(key, part):
    devices = NL // LEAF_DEV
    entries = LEAF_DEV * K0
    kinds = 2 * SLOT
    key_sets, key_extra, key_mix = jax.random.split(jax.random.fold_in(key, 11), 3)
    scores = jax.random.randint(key_sets, (devices, 2, LEAF_DEV), 0, 1 << 20) * LEAF_DEV + jnp.arange(LEAF_DEV, dtype=jnp.int32)
    chosen = jnp.argsort(scores, axis=-1, stable=True)[:, :, :SLOT].astype(jnp.int32)
    forced = jnp.broadcast_to(jnp.arange(kinds, dtype=jnp.int32)[None, :], (devices, kinds))
    extra = jax.random.randint(key_extra, (devices, entries - kinds), 0, 2 * kinds + LEAF_DEV).astype(jnp.int32)
    pooled = jnp.concatenate([forced, extra], axis=1)
    mixing = jax.vmap(lambda subkey: shuffled(subkey, entries))(jax.random.split(key_mix, devices))
    pooled = jnp.take_along_axis(pooled, mixing, axis=1)
    rows = jnp.arange(devices, dtype=jnp.int32)[:, None]
    is_side = pooled < 2 * kinds
    code = pooled % kinds
    side = code // SLOT
    within = code % SLOT
    picked = chosen[rows, side, within]
    neighbour = rows + 2 * side - 1
    valid = is_side & (neighbour >= 0) & (neighbour < devices)
    own_leaf = jnp.where(is_side, picked, pooled - 2 * kinds)
    leaf = jnp.where(valid, neighbour * LEAF_DEV + picked, rows * LEAF_DEV + own_leaf)
    return leaf.reshape(NL, K0).astype(jnp.int32)


def draw_mid_source(key, part):
    devices = NL1 // CHILD
    key_step, key_box, key_mix = jax.random.split(key, 3)
    home = jnp.arange(NL1, dtype=jnp.int32)[:, None] // CHILD
    moves = jax.random.randint(key_step, (NL1, K1), -1, 2).astype(jnp.int32)
    column = jnp.arange(K1, dtype=jnp.int32)[None, :]
    moves = jnp.where(column == 0, -1, jnp.where(column == 1, 1, moves))
    mixing = jax.vmap(lambda subkey: shuffled(subkey, K1))(jax.random.split(key_mix, NL1))
    moves = jnp.take_along_axis(moves, mixing, axis=1)
    target = home + moves
    target = jnp.where(target < 0, home + 1, jnp.where(target >= devices, home - 1, target))
    inside = jax.random.randint(key_box, (NL1, K1), 0, CHILD).astype(jnp.int32)
    return (target * CHILD + inside).astype(jnp.int32)


def draw_near_source(key, part):
    devices = NBALL // NB_CAP
    key_step, key_leaf, key_place = jax.random.split(key, 3)
    home = jnp.arange(NBALL, dtype=jnp.int32) // NB_CAP
    position = jnp.arange(NBALL, dtype=jnp.int32) % NB_CAP
    anchor = jax.random.randint(key_place, (devices,), 0, max(NB_CAP // 4 - 1, 1)).astype(jnp.int32)[home]
    moves = jax.random.randint(key_step, (NBALL,), -1, 2).astype(jnp.int32)
    moves = jnp.where(position == anchor, -1, jnp.where(position == anchor + 1, 1, moves))
    target = home + moves
    target = jnp.where(target < 0, home + 1, jnp.where(target >= devices, home - 1, target))
    inside = jax.random.randint(key_leaf, (NBALL,), 0, LEAF_DEV).astype(jnp.int32)
    return (target * LEAF_DEV + inside).astype(jnp.int32)


def draw_near_count(key, part):
    devices = NBALL // NB_CAP
    key_base, key_top = jax.random.split(key)
    base = jax.random.randint(key_base, (devices,), NB_CAP // 4, NB_CAP // 2 + 1).astype(jnp.int32)
    fullest = jax.random.randint(key_top, (), 0, devices).astype(jnp.int32)
    index = jnp.arange(devices, dtype=jnp.int32)
    full = (index == fullest) | (index == devices - 1)
    return jnp.where(full, NB_CAP, base).astype(jnp.int32)


def place_ends(result, key, low, top_value):
    shape = result.shape
    place = [jax.random.randint(jax.random.fold_in(key, axis), (), 0, shape[axis]) for axis in range(len(shape))]
    result = result.at[tuple(place)].set(low)
    longest = shape.index(max(shape))
    place[longest] = (place[longest] + 1) % shape[longest]
    return result.at[tuple(place)].set(top_value)


def steps_of(rng, dims, cuts, smallest, top_value):
    def one(axis_at, blocks):
        heights = jax.random.uniform(jax.random.fold_in(jax.random.fold_in(rng, 6), axis_at), (blocks,), jnp.float32, smallest / len(cuts), top_value / len(cuts))
        return jnp.repeat(jnp.exp(heights), dims[axis_at] // blocks).reshape((-1,) + (1,) * (len(dims) - axis_at - 1))

    level = one(*cuts[0])
    for cut in cuts[1:]:
        level = level * one(*cut)
    return level


def normal_values(key, shape, width, bound, pieces=(), kind=jnp.bfloat16):
    result = jax.random.normal(key, shape, jnp.float32) * width
    if len(pieces) > 0:
        result = steps_of(key, shape, pieces, -0.22, 0.18) * result
    return jnp.clip(result, min=-bound, max=bound).astype(kind)


def setup_inputs(seed: int = 0) -> dict:
    key_list = jax.random.split(jax.random.key(seed), 16)
    charges = normal_values(key_list[0], (NV, POINTS), 1.0, 6.0, ((1, 32),))
    leaf_basis = normal_values(key_list[1], (R0, POINTS), M ** -0.5, 0.75, ((1, 32),))
    leaf_transfer = normal_values(key_list[2], (NL1, R, CHILD * R0), (CHILD * R0) ** -0.5, 0.375, ((0, 32),))
    mid_transfer = normal_values(key_list[3], (BOXES, R, CHILD * R), (CHILD * R) ** -0.5, 0.25, ((0, 32),))
    far_source = draw_far_source(jax.random.fold_in(key_list[15], 71), 0)
    far_coupling = normal_values(key_list[5], (NL, R0, K0 * R0), (K0 * R0) ** -0.5, 0.25, ((0, 32),))
    mid_source = draw_mid_source(jax.random.fold_in(key_list[15], 71), 0)
    mid_coupling = normal_values(key_list[7], (NL1, R, K1 * R), (K1 * R) ** -0.5, 0.25, ((0, 32),))
    box_coupling = normal_values(key_list[8], (BOXES, R, 3 * R), (3 * R) ** -0.5, 0.4375, ((0, 32),))
    top_transfer = normal_values(key_list[9], (TOPS, R, 2 * R), (2 * R) ** -0.5, 0.5)
    top_coupling = normal_values(key_list[10], (TOPS, R, 3 * R), (3 * R) ** -0.5, 0.4375)
    near_target = place_ends(jax.random.randint(key_list[11], (NBALL,), 0, LEAF_DEV), jax.random.fold_in(key_list[11], 1), 0, LEAF_DEV - 1).astype(jnp.int32)
    near_source = draw_near_source(jax.random.fold_in(key_list[15], 71), 0)
    near_count = draw_near_count(jax.random.fold_in(key_list[15], 71), 0)
    near_blocks = normal_values(key_list[14], (M, NBALL * M), (8 * M) ** -0.5, 0.25, ((1, 32),))
    return dict(charges=charges, leaf_basis=leaf_basis, leaf_transfer=leaf_transfer, mid_transfer=mid_transfer, far_source=far_source, far_coupling=far_coupling, mid_source=mid_source, mid_coupling=mid_coupling, box_coupling=box_coupling, top_transfer=top_transfer, top_coupling=top_coupling, near_target=near_target, near_source=near_source, near_count=near_count, near_blocks=near_blocks)


deepest_level = lax.Precision.HIGHEST


def level_partners(upward):
    count = upward.shape[0]
    padded = jnp.pad(upward, ((3, 3), (0, 0), (0, 0)))
    is_even = (jnp.arange(count) % 2 == 0)[:, None, None]
    back_three = padded[0:count]
    back_two = padded[1:count + 1]
    ahead_two = padded[5:count + 5]
    ahead_three = padded[6:count + 6]
    return jnp.concatenate([jnp.where(is_even, back_two, back_three), jnp.where(is_even, ahead_two, back_two), jnp.where(is_even, ahead_three, ahead_two)], axis=1)


def reference(charges, leaf_basis, leaf_transfer, mid_transfer, far_source, far_coupling, mid_source, mid_coupling, box_coupling, top_transfer, top_coupling, near_target, near_source, near_count, near_blocks):
    leaves = NL
    groups = NL1
    charge_cube = charges.reshape(NV, leaves, M).astype(jnp.float32)
    basis_tensor = leaf_basis.reshape(R0, leaves, M).astype(jnp.float32)
    leaf_up = jnp.einsum('rlm,vlm->lrv', basis_tensor, charge_cube, precision=deepest_level).astype(jnp.bfloat16)
    mid_up = jnp.einsum('crk,ckv->crv', leaf_transfer.astype(jnp.float32), leaf_up.reshape(groups, CHILD * R0, NV).astype(jnp.float32), precision=deepest_level).astype(jnp.bfloat16)
    box_up = jnp.einsum('drk,dkv->drv', mid_transfer.astype(jnp.float32), mid_up.reshape(BOXES, CHILD * R, NV).astype(jnp.float32), precision=deepest_level)
    upward = [box_up]
    for level in range(LEVELS_TOP):
        count = BOXES >> (level + 1)
        start = BOXES - (BOXES >> level)
        parents = top_transfer[start:start + count].astype(jnp.float32)
        upward.append(jnp.einsum('prk,pkv->prv', parents, upward[-1].reshape(count, 2 * R, NV), precision=deepest_level))
    across = []
    for level in range(LEVELS_TOP + 1):
        count = BOXES >> level
        if level == 0:
            matrix_stack = box_coupling
        else:
            start = BOXES - (BOXES >> (level - 1))
            matrix_stack = top_coupling[start:start + count]
        across.append(jnp.einsum('crk,ckv->crv', matrix_stack.astype(jnp.float32), level_partners(upward[level]), precision=deepest_level))
    downward = across[LEVELS_TOP]
    for level in range(LEVELS_TOP - 1, -1, -1):
        count = BOXES >> (level + 1)
        start = BOXES - (BOXES >> level)
        parents = top_transfer[start:start + count].astype(jnp.float32)
        pushed = jnp.einsum('prk,prv->pkv', parents, downward, precision=deepest_level).reshape(2 * count, R, NV)
        downward = across[level] + pushed
    box_down = downward.astype(jnp.bfloat16)
    mid_picked = mid_up[mid_source].reshape(groups, K1 * R, NV).astype(jnp.float32)
    mid_far = jnp.einsum('crk,ckv->crv', mid_coupling.astype(jnp.float32), mid_picked, precision=deepest_level)
    mid_push = jnp.einsum('drk,drv->dkv', mid_transfer.astype(jnp.float32), box_down.astype(jnp.float32), precision=deepest_level).reshape(groups, R, NV)
    mid_down = (mid_far + mid_push).astype(jnp.bfloat16)
    leaf_picked = leaf_up[far_source].reshape(leaves, K0 * R0, NV).astype(jnp.float32)
    leaf_far = jnp.einsum('lrk,lkv->lrv', far_coupling.astype(jnp.float32), leaf_picked, precision=deepest_level)
    leaf_push = jnp.einsum('crk,crv->ckv', leaf_transfer.astype(jnp.float32), mid_down.astype(jnp.float32), precision=deepest_level).reshape(leaves, R0, NV)
    leaf_down = (leaf_far + leaf_push).astype(jnp.bfloat16)
    far_field = jnp.einsum('rlm,lrv->vlm', basis_tensor, leaf_down.astype(jnp.float32), precision=deepest_level)
    block = min(1024, NBALL)
    owners = jnp.arange(NBALL, dtype=jnp.int32) // NB_CAP
    alive = (jnp.arange(NBALL, dtype=jnp.int32) % NB_CAP) < near_count[owners]
    targets = (owners * LEAF_DEV + near_target).astype(jnp.int32)

    def near_step(step, total):
        first = (step * block).astype(jnp.int32)
        sources = lax.dynamic_slice_in_dim(near_source, first, block)
        dests = lax.dynamic_slice_in_dim(targets, first, block)
        weights = lax.dynamic_slice_in_dim(alive, first, block).astype(jnp.float32)
        dense = lax.dynamic_slice_in_dim(near_blocks, (first * M).astype(jnp.int32), block * M, 1).reshape(M, block, M).astype(jnp.float32)
        gathered = jnp.take(charge_cube, sources, axis=1)
        contribution = jnp.einsum('tbs,vbs->vbt', dense, gathered, precision=deepest_level) * weights[None, :, None]
        return total.at[:, dests, :].add(contribution)

    near_field = lax.fori_loop(0, NBALL // block, near_step, jnp.zeros((NV, leaves, M), jnp.float32))
    return (far_field + near_field).astype(jnp.bfloat16).reshape(NV, POINTS)
```

```python
import functools

import jax
import jax.numpy as jnp
from jax import lax
from jax.experimental import pallas as pl
from jax.experimental.pallas import tpu as pltpu
from jax.sharding import PartitionSpec as P

F32 = jnp.float32
BF16 = jnp.bfloat16
AXIS = "clusters"
NT = (((1,), (1,)), ((), ()))
NN = (((1,), (0,)), ((), ()))
LANES = 128
CHUNKS = 8


def dot_nt(a, b):
    return lax.dot_general(a, b, NT, preferred_element_type=F32)


def dot_nn(a, b):
    return lax.dot_general(a, b, NN, preferred_element_type=F32)


def lanes(shape):
    return lax.broadcasted_iota(jnp.int32, shape, len(shape) - 1)


def rows(shape):
    return lax.broadcasted_iota(jnp.int32, shape, len(shape) - 2)


def split(x):
    high = x.astype(BF16).astype(F32)
    return jnp.concatenate([high, x - high], axis=0).astype(BF16)


def exact_nt(x, matrix):
    v = x.shape[0]
    out = dot_nt(split(x), matrix)
    return out[:v] + out[v:]


def exact_nn(x, matrix):
    v = x.shape[0]
    out = dot_nn(split(x), matrix)
    return out[:v] + out[v:]


def diagonal(out, v, width):
    blocks = out.shape[0] // v
    lane = lanes((v, out.shape[1])) // width
    total = jnp.zeros((v, out.shape[1]), F32)
    for block in range(blocks):
        total = jnp.where(lane == block, out[block * v:(block + 1) * v], total)
    return total


def kernel(
    n, sizes,
    near_source, far_source, mid_source, near_count, near_target,
    charges_h, basis_h, leaf_transfer_h, mid_transfer_h, far_coupling_h, mid_coupling_h,
    box_coupling_h, top_transfer_h, top_coupling_h, near_blocks_h,
    out_ref,
    cw, lw, mw, gathered, basis, leaf_transfer, mid_transfer, far_coupling, mid_coupling,
    box_coupling, top_transfer, top_coupling, near_blocks,
    charge_tiles, leaf_tiles, mid_tiles, contribution, near_rows, leaf_far, mid_far, masked_basis, upward,
    load_sem, near_sem, top_sem, halo_send, halo_recv, all_send, all_recv,
):
    v, leaves, m, r0, groups, r, k0, k1, capacity = sizes
    child = leaves // groups
    levels = (n // 4).bit_length() - 1
    me = lax.axis_index(AXIS)
    half = lanes((v, LANES)) < m
    low_lane = lanes((v, LANES)) < r

    barrier = pltpu.get_barrier_semaphore()

    def greet(step, carry):
        other = lax.rem(me + step, n)
        pl.semaphore_signal(barrier, inc=1, device_id=(other,), device_id_type=pl.DeviceIdType.MESH)
        return carry

    lax.fori_loop(1, n, greet, 0)

    pairs = [
        (charges_h, cw.at[1]), (basis_h, basis), (leaf_transfer_h, leaf_transfer), (mid_transfer_h.at[0], mid_transfer),
        (mid_coupling_h, mid_coupling), (far_coupling_h, far_coupling), (box_coupling_h.at[0], box_coupling),
        (top_transfer_h, top_transfer),
    ]
    loads = [pltpu.make_async_copy(s, d, load_sem.at[i]) for i, (s, d) in enumerate(pairs)]
    width = near_blocks.shape[1] // CHUNKS

    def near_load(chunk):
        span = pl.ds(pl.multiple_of(chunk * width, width), width)
        return pltpu.make_async_copy(near_blocks_h.at[:, span], near_blocks.at[:, span], near_sem.at[chunk])

    for i in range(4):
        loads[i].start()
    for chunk in range(CHUNKS):
        near_load(chunk).start()
    for i in range(4, len(loads)):
        loads[i].start()
    tops = []
    for level in range(1, levels + 1):
        start = n - (n >> (level - 1))
        tops.append(pltpu.make_async_copy(
            top_coupling_h.at[start + (me >> level)], top_coupling.at[level - 1], top_sem.at[level - 1]))
    for copy in tops:
        copy.start()

    loads[0].wait()
    loads[1].wait()
    span_points = child * m
    lane_leaf = lanes((v, span_points)) // m
    ups = []
    for c in range(groups):
        x = cw[1, :, c * span_points:(c + 1) * span_points].astype(F32)
        lhs = jnp.concatenate([jnp.where(lane_leaf == l, x, 0.0) for l in range(child)], axis=0).astype(BF16)
        b = basis[:, c * span_points:(c + 1) * span_points]
        up = diagonal(dot_nt(lhs, jnp.concatenate([b] * child, axis=0)), v, r0).astype(BF16)
        lw[1, :, c * child * r0:(c + 1) * child * r0] = up
        ups.append(up.astype(F32))
    loads[2].wait()
    loads[3].wait()
    quad = 4
    for g in range(groups // quad):
        lhs = jnp.concatenate(ups[g * quad:(g + 1) * quad], axis=0).astype(BF16)
        matrix = leaf_transfer[g * quad:(g + 1) * quad].reshape(quad * r, child * r0)
        mw[1, :, g * quad * r:(g + 1) * quad * r] = diagonal(dot_nt(lhs, matrix), v, r).astype(BF16)
    transfer = mid_transfer[...]
    box_up = dot_nt(mw[1], jnp.concatenate([transfer, transfer], axis=0))
    gathered[me] = box_up

    pl.semaphore_wait(barrier, n - 1)

    def everyone(step):
        other = lax.rem(me + step, n)
        return pltpu.make_async_remote_copy(
            src_ref=gathered.at[me], dst_ref=gathered.at[me], send_sem=all_send.at[step],
            recv_sem=all_recv.at[me], device_id=(other,), device_id_type=pl.DeviceIdType.MESH)

    def arrival(source):
        return pltpu.make_async_remote_copy(
            src_ref=gathered.at[source], dst_ref=gathered.at[source], send_sem=all_send.at[0],
            recv_sem=all_recv.at[source], device_id=(me,), device_id_type=pl.DeviceIdType.MESH)

    wides = (cw, lw, mw)

    def halo(kind, side):
        wide = wides[kind]
        return pltpu.make_async_remote_copy(
            src_ref=wide.at[1], dst_ref=wide.at[2 - 2 * side], send_sem=halo_send.at[2 * kind + side],
            recv_sem=halo_recv.at[2 * kind + side], device_id=(me - 1 + 2 * side,),
            device_id_type=pl.DeviceIdType.MESH)

    def halo_starts(kind):
        @pl.when(me > 0)
        def _():
            halo(kind, 0).start()

        @pl.when(me < n - 1)
        def _():
            halo(kind, 1).start()

    def halo_arrive(kind):
        wide = wides[kind]

        @pl.when(me < n - 1)
        def _():
            halo(kind, 0).wait_recv()

        @pl.when(me > 0)
        def _():
            halo(kind, 1).wait_recv()

        @pl.when(me == 0)
        def _():
            wide[0] = jnp.zeros(wide.shape[1:], BF16)

        @pl.when(me == n - 1)
        def _():
            wide[2] = jnp.zeros(wide.shape[1:], BF16)

    def halo_sent(kind):
        @pl.when(me > 0)
        def _():
            halo(kind, 0).wait_send()

        @pl.when(me < n - 1)
        def _():
            halo(kind, 1).wait_send()

    halo_starts(0)

    def send_step(step, carry):
        everyone(step).start()
        return carry

    lax.fori_loop(1, n, send_step, 0)
    halo_starts(1)
    halo_starts(2)

    quad_mask = (rows((4 * r0, 4 * m)) // r0 == lanes((4 * r0, 4 * m)) // m).astype(F32).astype(BF16)
    for q in range(leaves // 4):
        b = basis[:, q * 4 * m:(q + 1) * 4 * m]
        masked_basis[q] = jnp.concatenate([b] * 4, axis=0) * quad_mask
    count = near_count[0]
    leaf_row = rows((leaves, LANES))
    slot_lane = lanes((leaves, LANES))
    assignment = []
    for b in range(capacity // LANES):
        hit = (leaf_row == near_target[b:b + 1, :]) & (slot_lane + b * LANES < count)
        assignment.append(jnp.where(hit, 1.0, 0.0).astype(BF16))

    def spread_pairs(wide, tiles, per_box, box):
        x = wide[box].astype(F32)
        first = lax.rem(me + 3 + box, 4) * per_box
        for t in range(per_box // 2):
            tile = x[:, t * LANES:(t + 1) * LANES]
            turned = pltpu.roll(tile, LANES // 2, 1)
            tiles[first + 2 * t] = jnp.where(half, tile, turned)
            tiles[first + 2 * t + 1] = jnp.where(half, turned, tile)

    fold = LANES // r0
    lane_block = lanes((v, LANES)) // r0

    def spread_leaves(box):
        x = lw[box].astype(F32)
        first = lax.rem(me + 3 + box, 4) * leaves
        for t in range(leaves // fold):
            tile = x[:, t * LANES:(t + 1) * LANES]
            turned = [tile] + [pltpu.roll(tile, r0 * k, 1) for k in range(1, fold)]
            for p in range(fold):
                piece = turned[(0 - p) % fold]
                for w in range(1, fold):
                    piece = jnp.where(lane_block == w, turned[(w - p) % fold], piece)
                leaf_tiles[first + t * fold + p] = piece

    for tiles, per_box in ((charge_tiles, leaves), (leaf_tiles, leaves), (mid_tiles, groups)):
        unused = pl.ds(lax.rem(me + 2, 4) * per_box, per_box)
        tiles[unused] = jnp.zeros((per_box, v, LANES), F32)
    spread_pairs(cw, charge_tiles, leaves, 1)
    halo_arrive(0)
    spread_pairs(cw, charge_tiles, leaves, 0)
    spread_pairs(cw, charge_tiles, leaves, 2)

    block = 32
    zero = jnp.zeros((2 * v, LANES), F32)
    steps_per_chunk = capacity // CHUNKS // block

    def near_step(step, carry):
        base = step * block
        for g in range(block // 4):
            pieces = []
            for i in range(4):
                x = charge_tiles[near_source[base + g * 4 + i] & (4 * leaves - 1)]
                pieces.append(jnp.where(half, x, 0.0) if i % 2 == 0 else jnp.where(half, 0.0, x))
            upper = jnp.concatenate([pieces[0], pieces[1]], axis=0)
            lower = jnp.concatenate([pieces[2], pieces[3]], axis=0)
            lhs = jnp.concatenate(
                [jnp.concatenate([upper, zero], axis=1), jnp.concatenate([zero, lower], axis=1)], axis=0).astype(BF16)
            span = pl.ds(pl.multiple_of(base * m + g * 4 * m, 4 * m), 4 * m)
            contribution[pl.ds(pl.multiple_of((base + g * 4) * v, 4 * v), 4 * v), :] = dot_nt(lhs, near_blocks[:, span])
        return carry

    def near_chunk(chunk, carry):
        near_load(chunk).wait()
        return lax.fori_loop(chunk * steps_per_chunk, (chunk + 1) * steps_per_chunk, near_step, carry)

    lax.fori_loop(0, CHUNKS, near_chunk, 0)

    for u in range(v):
        total = jnp.zeros((leaves, 2 * m), F32)
        for b in range(capacity // LANES):
            c = contribution[pl.ds(b * LANES * v + u, LANES, stride=v), :]
            high = c.astype(BF16)
            low = (c - high.astype(F32)).astype(BF16)
            total = total + dot_nn(assignment[b], jnp.concatenate([high, low], axis=1))
        near_rows[u * leaves:(u + 1) * leaves, :] = total

    halo_arrive(1)
    for box in range(3):
        spread_leaves(box)
    loads[5].wait()

    def far_step(c, carry):
        parts = []
        for l in range(child):
            tiles = []
            for t in range(k0 // fold):
                piece = leaf_tiles[far_source[c * child + l, t * fold] & (4 * leaves - 1)]
                for w in range(1, fold):
                    source = far_source[c * child + l, t * fold + w] & (4 * leaves - 1)
                    piece = jnp.where(lane_block == w, leaf_tiles[source], piece)
                tiles.append(piece)
            parts.append(jnp.concatenate(tiles, axis=1))
        lhs = jnp.concatenate(parts, axis=0).astype(BF16)
        matrix = far_coupling[pl.ds(c * child, child)].reshape(child * r0, k0 * r0)
        leaf_far[c] = diagonal(dot_nt(lhs, matrix), v, r0)
        return carry

    lax.fori_loop(0, groups, far_step, 0)

    halo_arrive(2)
    for box in range(3):
        spread_pairs(mw, mid_tiles, groups, box)
    loads[4].wait()
    for g in range(groups // quad):
        parts = []
        for c in range(g * quad, (g + 1) * quad):
            tiles = []
            for t in range(k1 // 2):
                a = mid_tiles[mid_source[c, 2 * t] & (4 * groups - 1)]
                b = mid_tiles[mid_source[c, 2 * t + 1] & (4 * groups - 1)]
                tiles.append(jnp.where(half, a, b))
            parts.append(jnp.concatenate(tiles, axis=1))
        lhs = jnp.concatenate(parts, axis=0).astype(BF16)
        matrix = mid_coupling[g * quad:(g + 1) * quad].reshape(quad * r, k1 * r)
        mid_far[:, g * quad * r:(g + 1) * quad * r] = diagonal(dot_nt(lhs, matrix), v, r)

    loads[6].wait()
    loads[7].wait()
    for copy in tops:
        copy.wait()

    def arrive_step(step, carry):
        arrival(lax.rem(me + step, n)).wait_recv()
        return carry

    lax.fori_loop(1, n, arrive_step, 0)

    offset = 0
    for level in range(levels):
        size = n >> level
        start = n - size
        below = gathered if level == 0 else upward
        for q in range(size // 2):
            a = below[offset + 2 * q]
            b = below[offset + 2 * q + 1]
            t = top_transfer[start + q]
            upward[start + q] = exact_nt(jnp.where(low_lane, a, b), jnp.concatenate([t, t], axis=0))
        offset = start
    across = []
    for level in range(levels + 1):
        size = n >> level
        cluster = me >> level
        below = gathered if level == 0 else upward
        base = 0 if level == 0 else n - (n >> (level - 1))
        odd = lax.rem(cluster, 2)
        found = []
        for partner in (cluster - 2 - odd, cluster + 2 - 4 * odd, cluster + 3 - odd):
            inside = (partner >= 0) & (partner < size)
            safe = jnp.clip(partner, 0, size - 1)
            found.append(below[base + safe] * jnp.where(inside, 1.0, 0.0))
        g = box_coupling[...] if level == 0 else top_coupling[level - 1]
        g = jnp.concatenate([g, g], axis=0)
        across.append(exact_nt(jnp.where(low_lane, found[0], found[1]), g[:, :2 * r])
                      + exact_nt(found[2][:, :r], g[:, 2 * r:]))
    downward = across[levels]
    for level in range(levels - 1, -1, -1):
        cluster = me >> level
        start = n - (n >> level)
        pushed = exact_nn(downward[:, :r], top_transfer[start + (cluster >> 1)])
        turned = pltpu.roll(pushed, LANES // 2, 1)
        left = jnp.where(low_lane, pushed, turned)
        right = jnp.where(low_lane, turned, pushed)
        odd = lax.rem(cluster, 2).astype(F32)
        downward = across[level] + left * (1.0 - odd) + right * odd

    mid_push = dot_nn(downward[:, :r].astype(BF16), mid_transfer[...])
    mid_down = (mid_far[...] + mid_push).astype(BF16).astype(F32)
    near_half = lanes((v, LANES)) < m
    for pair in range(groups // 2):
        tile = mid_down[:, pair * LANES:(pair + 1) * LANES]
        lhs = jnp.concatenate([jnp.where(low_lane, tile, 0.0), jnp.where(low_lane, 0.0, tile)], axis=0).astype(BF16)
        matrix = leaf_transfer[2 * pair:2 * pair + 2].reshape(2 * r, child * r0)
        push = dot_nn(lhs, matrix)
        for s in range(2):
            c = 2 * pair + s
            leaf_down = (leaf_far[c] + push[s * v:(s + 1) * v]).astype(BF16)
            for h in range(child // 4):
                q = c * (child // 4) + h
                far = dot_nn(leaf_down[:, h * 4 * r0:(h + 1) * 4 * r0], masked_basis[q])
                for w in range(2):
                    leaf = q * 4 + 2 * w
                    a = near_rows[pl.ds(leaf, v, stride=leaves), :]
                    b = near_rows[pl.ds(leaf + 1, v, stride=leaves), :]
                    a = a + pltpu.roll(a, m, 1)
                    b = b + pltpu.roll(b, m, 1)
                    near = jnp.where(near_half, a, b)
                    out_ref[:, leaf * m:(leaf + 2) * m] = (far[:, w * LANES:(w + 1) * LANES] + near).astype(BF16)

    def sent_step(step, carry):
        everyone(step).wait_send()
        return carry

    lax.fori_loop(1, n, sent_step, 0)
    for kind in range(3):
        halo_sent(kind)


def body(
    charges, leaf_basis, leaf_transfer, mid_transfer, far_source, far_coupling, mid_source, mid_coupling,
    box_coupling, top_transfer, top_coupling, near_target, near_source, near_count, near_blocks,
):
    n = lax.axis_size(AXIS)
    v, points = charges.shape
    leaves, k0 = far_source.shape
    m = points // leaves
    r0 = leaf_basis.shape[0]
    groups, k1 = mid_source.shape
    r = leaf_transfer.shape[1]
    capacity = near_target.shape[0]
    levels = (n // 4).bit_length() - 1
    sizes = (v, leaves, m, r0, groups, r, k0, k1, capacity)
    smem = pl.BlockSpec(memory_space=pltpu.SMEM)
    vmem = pl.BlockSpec(memory_space=pltpu.VMEM)
    hbm = pl.BlockSpec(memory_space=pl.ANY)
    dma = pltpu.SemaphoreType.DMA
    return pl.pallas_call(
        functools.partial(kernel, n, sizes),
        out_shape=jax.ShapeDtypeStruct(charges.shape, BF16),
        in_specs=[smem, smem, smem, smem, vmem] + [hbm] * 10,
        out_specs=vmem,
        scratch_shapes=[
            pltpu.VMEM((3, v, points), BF16),
            pltpu.VMEM((3, v, leaves * r0), BF16),
            pltpu.VMEM((3, v, groups * r), BF16),
            pltpu.VMEM((n, v, 2 * r), F32),
            pltpu.VMEM(leaf_basis.shape, BF16),
            pltpu.VMEM(leaf_transfer.shape, BF16),
            pltpu.VMEM(mid_transfer.shape[1:], BF16),
            pltpu.VMEM(far_coupling.shape, BF16),
            pltpu.VMEM(mid_coupling.shape, BF16),
            pltpu.VMEM(box_coupling.shape[1:], BF16),
            pltpu.VMEM(top_transfer.shape, BF16),
            pltpu.VMEM((levels,) + top_coupling.shape[1:], BF16),
            pltpu.VMEM(near_blocks.shape, BF16),
            pltpu.VMEM((4 * leaves, v, LANES), F32),
            pltpu.VMEM((4 * leaves, v, LANES), F32),
            pltpu.VMEM((4 * groups, v, LANES), F32),
            pltpu.VMEM((capacity * v, m), F32),
            pltpu.VMEM((v * leaves, 2 * m), F32),
            pltpu.VMEM((groups, v, leaves // groups * r0), F32),
            pltpu.VMEM((v, groups * r), F32),
            pltpu.VMEM((leaves // 4, 4 * r0, 4 * m), BF16),
            pltpu.VMEM((n, v, 2 * r), F32),
            dma((8,)),
            dma((CHUNKS,)),
            dma((levels,)),
            dma((6,)),
            dma((6,)),
            dma((n,)),
            dma((n,)),
        ],
        compiler_params=pltpu.CompilerParams(
            collective_id=0, has_side_effects=True, vmem_limit_bytes=60 * 1024 * 1024),
    )(
        near_source, far_source, mid_source, near_count, near_target.reshape(capacity // LANES, LANES),
        charges, leaf_basis, leaf_transfer, mid_transfer, far_coupling, mid_coupling,
        box_coupling, top_transfer, top_coupling, near_blocks,
    )


def solution(mesh):
    c = "clusters"
    in_specs = (
        P(None, c), P(None, c), P(c, None, None), P(c, None, None), P(c, None), P(c, None, None),
        P(c, None), P(c, None, None), P(c, None, None), P(), P(), P(c), P(c), P(c), P(None, c),
    )
    return jax.shard_map(body, mesh=mesh, in_specs=in_specs, out_specs=P(None, c), check_vma=False)
```

```python
import functools

import jax
import jax.numpy as jnp
from jax import lax
from jax.experimental import pallas as pl
from jax.experimental.pallas import tpu as pltpu
from jax.sharding import PartitionSpec as P

F32 = jnp.float32
BF16 = jnp.bfloat16
AXIS = "clusters"
NT = (((1,), (1,)), ((), ()))
NN = (((1,), (0,)), ((), ()))
LANES = 128
CHUNKS = 8


def dot_nt(a, b):
    return lax.dot_general(a, b, NT, preferred_element_type=F32)


def dot_nn(a, b):
    return lax.dot_general(a, b, NN, preferred_element_type=F32)


def lanes(shape):
    return lax.broadcasted_iota(jnp.int32, shape, len(shape) - 1)


def rows(shape):
    return lax.broadcasted_iota(jnp.int32, shape, len(shape) - 2)


def split(x):
    high = x.astype(BF16).astype(F32)
    return jnp.concatenate([high, x - high], axis=0).astype(BF16)


def exact_nt(x, matrix):
    v = x.shape[0]
    out = dot_nt(split(x), matrix)
    return out[:v] + out[v:]


def exact_nn(x, matrix):
    v = x.shape[0]
    out = dot_nn(split(x), matrix)
    return out[:v] + out[v:]


def diagonal(out, v, width):
    blocks = out.shape[0] // v
    lane = lanes((v, out.shape[1])) // width
    total = jnp.zeros((v, out.shape[1]), F32)
    for block in range(blocks):
        total = jnp.where(lane == block, out[block * v:(block + 1) * v], total)
    return total


def kernel(
    n, sizes,
    near_source, far_source, mid_source, near_count, near_target,
    charges_h, basis_h, leaf_transfer_h, mid_transfer_h, far_coupling_h, mid_coupling_h,
    box_coupling_h, top_transfer_h, top_coupling_h, near_blocks_h,
    out_ref,
    cw, lw, mw, gathered, basis, leaf_transfer, mid_transfer, far_coupling, mid_coupling,
    box_coupling, top_transfer, top_coupling, near_blocks,
    charge_tiles, leaf_tiles, mid_tiles, contribution, near_rows, leaf_far, mid_far, masked_basis, upward, assigned,
    load_sem, near_sem, top_sem, halo_send, halo_recv, all_send, all_recv,
):
    v, leaves, m, r0, groups, r, k0, k1, capacity = sizes
    child = leaves // groups
    levels = (n // 4).bit_length() - 1
    me = lax.axis_index(AXIS)
    half = lanes((v, LANES)) < m
    low_lane = lanes((v, LANES)) < r

    barrier = pltpu.get_barrier_semaphore()

    pairs = [
        (charges_h, cw.at[1]), (basis_h, basis), (leaf_transfer_h, leaf_transfer), (mid_transfer_h.at[0], mid_transfer),
        (mid_coupling_h, mid_coupling), (far_coupling_h, far_coupling), (box_coupling_h.at[0], box_coupling),
        (top_transfer_h, top_transfer),
    ]
    loads = [pltpu.make_async_copy(s, d, load_sem.at[i]) for i, (s, d) in enumerate(pairs)]
    width = near_blocks.shape[1] // CHUNKS

    def near_load(chunk):
        span = pl.ds(pl.multiple_of(chunk * width, width), width)
        return pltpu.make_async_copy(near_blocks_h.at[:, span], near_blocks.at[:, span], near_sem.at[chunk])

    for i in range(4):
        loads[i].start()
    for chunk in range(CHUNKS):
        near_load(chunk).start()
    for i in range(4, len(loads)):
        loads[i].start()
    tops = []
    for level in range(1, levels + 1):
        start = n - (n >> (level - 1))
        tops.append(pltpu.make_async_copy(
            top_coupling_h.at[start + (me >> level)], top_coupling.at[level - 1], top_sem.at[level - 1]))
    for copy in tops:
        copy.start()

    def greet(step, carry):
        other = lax.rem(me + step, n)
        pl.semaphore_signal(barrier, inc=1, device_id=(other,), device_id_type=pl.DeviceIdType.MESH)
        return carry

    lax.fori_loop(1, n, greet, 0)

    loads[0].wait()
    loads[1].wait()
    span_points = child * m
    lane_leaf = lanes((v, span_points)) // m
    ups = []
    for c in range(groups):
        x = cw[1, :, c * span_points:(c + 1) * span_points].astype(F32)
        lhs = jnp.concatenate([jnp.where(lane_leaf == l, x, 0.0) for l in range(child)], axis=0).astype(BF16)
        b = basis[:, c * span_points:(c + 1) * span_points]
        up = diagonal(dot_nt(lhs, jnp.concatenate([b] * child, axis=0)), v, r0).astype(BF16)
        lw[1, :, c * child * r0:(c + 1) * child * r0] = up
        ups.append(up.astype(F32))
    loads[2].wait()
    loads[3].wait()
    quad = 4
    for g in range(groups // quad):
        lhs = jnp.concatenate(ups[g * quad:(g + 1) * quad], axis=0).astype(BF16)
        matrix = leaf_transfer[g * quad:(g + 1) * quad].reshape(quad * r, child * r0)
        mw[1, :, g * quad * r:(g + 1) * quad * r] = diagonal(dot_nt(lhs, matrix), v, r).astype(BF16)
    transfer = mid_transfer[...]
    box_up = dot_nt(mw[1], jnp.concatenate([transfer, transfer], axis=0))
    gathered[me] = box_up

    quad_mask = (rows((4 * r0, 4 * m)) // r0 == lanes((4 * r0, 4 * m)) // m).astype(F32).astype(BF16)
    for q in range(leaves // 4):
        b = basis[:, q * 4 * m:(q + 1) * 4 * m]
        masked_basis[q] = jnp.concatenate([b] * 4, axis=0) * quad_mask
    count = near_count[0]
    leaf_row = rows((leaves, LANES))
    slot_lane = lanes((leaves, LANES))
    assignment = []
    for b in range(capacity // LANES):
        hit = (leaf_row == near_target[b:b + 1, :]) & (slot_lane + b * LANES < count)
        assignment.append(jnp.where(hit, 1.0, 0.0).astype(BF16))
    assignment = [jnp.concatenate(assignment[b:b + 2], axis=1) for b in range(0, len(assignment), 2)]
    for b, value in enumerate(assignment):
        assigned[b] = value

    def spread_pairs(wide, tiles, per_box, box):
        x = wide[box].astype(F32)
        first = lax.rem(me + 3 + box, 4) * per_box
        for t in range(per_box // 2):
            tile = x[:, t * LANES:(t + 1) * LANES]
            turned = pltpu.roll(tile, LANES // 2, 1)
            tiles[first + 2 * t] = jnp.where(half, tile, turned)
            tiles[first + 2 * t + 1] = jnp.where(half, turned, tile)

    fold = LANES // r0
    lane_block = lanes((v, LANES)) // r0

    def spread_leaves(box):
        x = lw[box].astype(F32)
        first = lax.rem(me + 3 + box, 4) * leaves
        for t in range(leaves // fold):
            tile = x[:, t * LANES:(t + 1) * LANES]
            turned = [tile] + [pltpu.roll(tile, r0 * k, 1) for k in range(1, fold)]
            for p in range(fold):
                piece = turned[(0 - p) % fold]
                for w in range(1, fold):
                    piece = jnp.where(lane_block == w, turned[(w - p) % fold], piece)
                leaf_tiles[first + t * fold + p] = piece

    for tiles, per_box in ((charge_tiles, leaves), (leaf_tiles, leaves), (mid_tiles, groups)):
        unused = pl.ds(lax.rem(me + 2, 4) * per_box, per_box)
        tiles[unused] = jnp.zeros((per_box, v, LANES), F32)
    spread_pairs(cw, charge_tiles, leaves, 1)
    spread_leaves(1)
    spread_pairs(mw, mid_tiles, groups, 1)

    pl.semaphore_wait(barrier, n - 1)

    def everyone(step):
        other = lax.rem(me + step, n)
        return pltpu.make_async_remote_copy(
            src_ref=gathered.at[me], dst_ref=gathered.at[me], send_sem=all_send.at[step],
            recv_sem=all_recv.at[me], device_id=(other,), device_id_type=pl.DeviceIdType.MESH)

    def arrival(source):
        return pltpu.make_async_remote_copy(
            src_ref=gathered.at[source], dst_ref=gathered.at[source], send_sem=all_send.at[0],
            recv_sem=all_recv.at[source], device_id=(me,), device_id_type=pl.DeviceIdType.MESH)

    wides = (cw, lw, mw)

    def halo(kind, side):
        wide = wides[kind]
        return pltpu.make_async_remote_copy(
            src_ref=wide.at[1], dst_ref=wide.at[2 - 2 * side], send_sem=halo_send.at[2 * kind + side],
            recv_sem=halo_recv.at[2 * kind + side], device_id=(me - 1 + 2 * side,),
            device_id_type=pl.DeviceIdType.MESH)

    def halo_starts(kind):
        @pl.when(me > 0)
        def _():
            halo(kind, 0).start()

        @pl.when(me < n - 1)
        def _():
            halo(kind, 1).start()

    def halo_arrive(kind):
        wide = wides[kind]

        @pl.when(me < n - 1)
        def _():
            halo(kind, 0).wait_recv()

        @pl.when(me > 0)
        def _():
            halo(kind, 1).wait_recv()

        @pl.when(me == 0)
        def _():
            wide[0] = jnp.zeros(wide.shape[1:], BF16)

        @pl.when(me == n - 1)
        def _():
            wide[2] = jnp.zeros(wide.shape[1:], BF16)

    def halo_sent(kind):
        @pl.when(me > 0)
        def _():
            halo(kind, 0).wait_send()

        @pl.when(me < n - 1)
        def _():
            halo(kind, 1).wait_send()

    def send_step(step, carry):
        everyone(step).start()
        return carry

    halo_starts(1)
    halo_starts(0)
    halo_starts(2)
    lax.fori_loop(1, n, send_step, 0)

    halo_arrive(1)
    spread_leaves(0)
    spread_leaves(2)
    loads[5].wait()

    def far_step(c, carry):
        parts = []
        for l in range(child):
            tiles = []
            for t in range(k0 // fold):
                piece = leaf_tiles[far_source[t * fold, c * child + l] & (4 * leaves - 1)]
                for w in range(1, fold):
                    source = far_source[t * fold + w, c * child + l] & (4 * leaves - 1)
                    piece = jnp.where(lane_block == w, leaf_tiles[source], piece)
                tiles.append(piece)
            parts.append(jnp.concatenate(tiles, axis=1))
        lhs = jnp.concatenate(parts, axis=0).astype(BF16)
        matrix = far_coupling[c * child:(c + 1) * child].reshape(child * r0, k0 * r0)
        leaf_far[c] = diagonal(dot_nt(lhs, matrix), v, r0)
        return carry

    for c in range(groups):
        far_step(c, 0)

    halo_arrive(0)
    spread_pairs(cw, charge_tiles, leaves, 0)
    spread_pairs(cw, charge_tiles, leaves, 2)

    zero = jnp.zeros((2 * v, LANES), F32)

    for g in range(capacity // 4):
        if g % (capacity // 4 // CHUNKS) == 0:
            near_load(g // (capacity // 4 // CHUNKS)).wait()
        pieces = []
        for i in range(4):
            x = charge_tiles[near_source[g * 4 + i] & (4 * leaves - 1)]
            pieces.append(jnp.where(half, x, 0.0) if i % 2 == 0 else jnp.where(half, 0.0, x))
        upper = jnp.concatenate([pieces[0], pieces[1]], axis=0)
        lower = jnp.concatenate([pieces[2], pieces[3]], axis=0)
        lhs = jnp.concatenate(
            [jnp.concatenate([upper, zero], axis=1), jnp.concatenate([zero, lower], axis=1)], axis=0).astype(BF16)
        contribution[g * 4 * v:(g + 1) * 4 * v, :] = dot_nt(lhs, near_blocks[:, g * 4 * m:(g + 1) * 4 * m])

    for u in range(v):
        total = jnp.zeros((leaves, m), F32)
        for b in range(capacity // LANES // 2):
            c = contribution[pl.ds(b * 2 * LANES * v + u, 2 * LANES, stride=v), :]
            total = total + dot_nn(assigned[b], c.astype(BF16))
        near_rows[u * leaves:(u + 1) * leaves, :] = jnp.concatenate([total, total], axis=1)

    halo_arrive(2)
    spread_pairs(mw, mid_tiles, groups, 0)
    spread_pairs(mw, mid_tiles, groups, 2)
    loads[4].wait()
    for g in range(groups // quad):
        parts = []
        for c in range(g * quad, (g + 1) * quad):
            tiles = []
            for t in range(k1 // 2):
                a = mid_tiles[mid_source[c, 2 * t] & (4 * groups - 1)]
                b = mid_tiles[mid_source[c, 2 * t + 1] & (4 * groups - 1)]
                tiles.append(jnp.where(half, a, b))
            parts.append(jnp.concatenate(tiles, axis=1))
        lhs = jnp.concatenate(parts, axis=0).astype(BF16)
        matrix = mid_coupling[g * quad:(g + 1) * quad].reshape(quad * r, k1 * r)
        mid_far[:, g * quad * r:(g + 1) * quad * r] = diagonal(dot_nt(lhs, matrix), v, r)

    loads[6].wait()
    loads[7].wait()
    for copy in tops:
        copy.wait()

    def arrive_step(step, carry):
        arrival(lax.rem(me + step, n)).wait_recv()
        return carry

    lax.fori_loop(1, n, arrive_step, 0)

    offset = 0
    for level in range(levels):
        size = n >> level
        start = n - size
        below = gathered if level == 0 else upward
        for q in range(size // 2):
            a = below[offset + 2 * q]
            b = below[offset + 2 * q + 1]
            t = top_transfer[start + q]
            upward[start + q] = exact_nt(jnp.where(low_lane, a, b), jnp.concatenate([t, t], axis=0))
        offset = start
    across = []
    for level in range(levels + 1):
        size = n >> level
        cluster = me >> level
        below = gathered if level == 0 else upward
        base = 0 if level == 0 else n - (n >> (level - 1))
        odd = lax.rem(cluster, 2)
        found = []
        for partner in (cluster - 2 - odd, cluster + 2 - 4 * odd, cluster + 3 - odd):
            inside = (partner >= 0) & (partner < size)
            safe = jnp.clip(partner, 0, size - 1)
            found.append(below[base + safe] * jnp.where(inside, 1.0, 0.0))
        g = box_coupling[...] if level == 0 else top_coupling[level - 1]
        g = jnp.concatenate([g, g], axis=0)
        across.append(exact_nt(jnp.where(low_lane, found[0], found[1]), g[:, :2 * r])
                      + exact_nt(found[2][:, :r], g[:, 2 * r:]))
    downward = across[levels]
    for level in range(levels - 1, -1, -1):
        cluster = me >> level
        start = n - (n >> level)
        pushed = exact_nn(downward[:, :r], top_transfer[start + (cluster >> 1)])
        turned = pltpu.roll(pushed, LANES // 2, 1)
        left = jnp.where(low_lane, pushed, turned)
        right = jnp.where(low_lane, turned, pushed)
        odd = lax.rem(cluster, 2).astype(F32)
        downward = across[level] + left * (1.0 - odd) + right * odd

    mid_push = dot_nn(downward[:, :r].astype(BF16), mid_transfer[...])
    mid_down = (mid_far[...] + mid_push).astype(BF16).astype(F32)
    near_half = lanes((v, LANES)) < m
    for pair in range(groups // 2):
        tile = mid_down[:, pair * LANES:(pair + 1) * LANES]
        lhs = jnp.concatenate([jnp.where(low_lane, tile, 0.0), jnp.where(low_lane, 0.0, tile)], axis=0).astype(BF16)
        matrix = leaf_transfer[2 * pair:2 * pair + 2].reshape(2 * r, child * r0)
        push = dot_nn(lhs, matrix)
        for s in range(2):
            c = 2 * pair + s
            leaf_down = (leaf_far[c] + push[s * v:(s + 1) * v]).astype(BF16)
            for h in range(child // 4):
                q = c * (child // 4) + h
                far = dot_nn(leaf_down[:, h * 4 * r0:(h + 1) * 4 * r0], masked_basis[q])
                for w in range(2):
                    leaf = q * 4 + 2 * w
                    a = near_rows[pl.ds(leaf, v, stride=leaves), :]
                    b = near_rows[pl.ds(leaf + 1, v, stride=leaves), :]
                    near = jnp.where(near_half, a, b)
                    out_ref[:, leaf * m:(leaf + 2) * m] = (far[:, w * LANES:(w + 1) * LANES] + near).astype(BF16)

    def sent_step(step, carry):
        everyone(step).wait_send()
        return carry

    lax.fori_loop(1, n, sent_step, 0)
    for kind in range(3):
        halo_sent(kind)


def body(
    charges, leaf_basis, leaf_transfer, mid_transfer, far_source, far_coupling, mid_source, mid_coupling,
    box_coupling, top_transfer, top_coupling, near_target, near_source, near_count, near_blocks,
):
    n = lax.axis_size(AXIS)
    v, points = charges.shape
    leaves, k0 = far_source.shape
    m = points // leaves
    r0 = leaf_basis.shape[0]
    groups, k1 = mid_source.shape
    r = leaf_transfer.shape[1]
    capacity = near_target.shape[0]
    levels = (n // 4).bit_length() - 1
    sizes = (v, leaves, m, r0, groups, r, k0, k1, capacity)
    smem = pl.BlockSpec(memory_space=pltpu.SMEM)
    vmem = pl.BlockSpec(memory_space=pltpu.VMEM)
    hbm = pl.BlockSpec(memory_space=pl.ANY)
    dma = pltpu.SemaphoreType.DMA
    return pl.pallas_call(
        functools.partial(kernel, n, sizes),
        out_shape=jax.ShapeDtypeStruct(charges.shape, BF16),
        in_specs=[smem, smem, smem, smem, vmem] + [hbm] * 10,
        out_specs=vmem,
        scratch_shapes=[
            pltpu.VMEM((3, v, points), BF16),
            pltpu.VMEM((3, v, leaves * r0), BF16),
            pltpu.VMEM((3, v, groups * r), BF16),
            pltpu.VMEM((n, v, 2 * r), F32),
            pltpu.VMEM(leaf_basis.shape, BF16),
            pltpu.VMEM(leaf_transfer.shape, BF16),
            pltpu.VMEM(mid_transfer.shape[1:], BF16),
            pltpu.VMEM(far_coupling.shape, BF16),
            pltpu.VMEM(mid_coupling.shape, BF16),
            pltpu.VMEM(box_coupling.shape[1:], BF16),
            pltpu.VMEM(top_transfer.shape, BF16),
            pltpu.VMEM((levels,) + top_coupling.shape[1:], BF16),
            pltpu.VMEM(near_blocks.shape, BF16),
            pltpu.VMEM((4 * leaves, v, LANES), F32),
            pltpu.VMEM((4 * leaves, v, LANES), F32),
            pltpu.VMEM((4 * groups, v, LANES), F32),
            pltpu.VMEM((capacity * v, m), F32),
            pltpu.VMEM((v * leaves, 2 * m), F32),
            pltpu.VMEM((groups, v, leaves // groups * r0), F32),
            pltpu.VMEM((v, groups * r), F32),
            pltpu.VMEM((leaves // 4, 4 * r0, 4 * m), BF16),
            pltpu.VMEM((n, v, 2 * r), F32),
            pltpu.VMEM((capacity // LANES // 2, leaves, 2 * LANES), BF16),
            dma((8,)),
            dma((CHUNKS,)),
            dma((levels,)),
            dma((6,)),
            dma((6,)),
            dma((n,)),
            dma((n,)),
        ],
        compiler_params=pltpu.CompilerParams(
            collective_id=0, has_side_effects=True, vmem_limit_bytes=60 * 1024 * 1024),
    )(
        near_source, far_source.T, mid_source, near_count, near_target.reshape(capacity // LANES, LANES),
        charges, leaf_basis, leaf_transfer, mid_transfer, far_coupling, mid_coupling,
        box_coupling, top_transfer, top_coupling, near_blocks,
    )


def solution(mesh):
    c = "clusters"
    in_specs = (
        P(None, c), P(None, c), P(c, None, None), P(c, None, None), P(c, None), P(c, None, None),
        P(c, None), P(c, None, None), P(c, None, None), P(), P(), P(c), P(c), P(c), P(None, c),
    )
    return jax.shard_map(body, mesh=mesh, in_specs=in_specs, out_specs=P(None, c), check_vma=False)
```

```python
import functools

import jax
import jax.numpy as jnp
from jax import lax
from jax.experimental import pallas as pl
from jax.experimental.pallas import tpu as pltpu
from jax.sharding import PartitionSpec as P

F32 = jnp.float32
BF16 = jnp.bfloat16
AXIS = "clusters"
NT = (((1,), (1,)), ((), ()))
NN = (((1,), (0,)), ((), ()))
LANES = 128
CHUNKS = 8


def dot_nt(a, b):
    return lax.dot_general(a, b, NT, preferred_element_type=F32)


def dot_nn(a, b):
    return lax.dot_general(a, b, NN, preferred_element_type=F32)


def lanes(shape):
    return lax.broadcasted_iota(jnp.int32, shape, len(shape) - 1)


def rows(shape):
    return lax.broadcasted_iota(jnp.int32, shape, len(shape) - 2)


def split(x):
    high = x.astype(BF16).astype(F32)
    return jnp.concatenate([high, x - high], axis=0).astype(BF16)


def exact_nt(x, matrix):
    v = x.shape[0]
    out = dot_nt(split(x), matrix)
    return out[:v] + out[v:]


def exact_nn(x, matrix):
    v = x.shape[0]
    out = dot_nn(split(x), matrix)
    return out[:v] + out[v:]


def diagonal(out, v, width):
    blocks = out.shape[0] // v
    lane = lanes((v, out.shape[1])) // width
    total = jnp.zeros((v, out.shape[1]), F32)
    for block in range(blocks):
        total = jnp.where(lane == block, out[block * v:(block + 1) * v], total)
    return total


def kernel(
    n, sizes,
    near_source, far_source, mid_source, near_count, near_target,
    charges_h, basis_h, leaf_transfer_h, mid_transfer_h, far_coupling_h, mid_coupling_h,
    box_coupling_h, top_transfer_h, top_coupling_h, near_blocks_h,
    out_ref,
    cw, lw, mw, gathered, basis, leaf_transfer, mid_transfer, far_coupling, mid_coupling,
    box_coupling, top_transfer, top_coupling, near_blocks,
    charge_tiles, leaf_tiles, mid_tiles, contribution, near_rows, leaf_far, mid_far, masked_basis, upward, assigned,
    load_sem, near_sem, top_sem, halo_send, halo_recv, all_send, all_recv,
):
    v, leaves, m, r0, groups, r, k0, k1, capacity = sizes
    child = leaves // groups
    levels = (n // 4).bit_length() - 1
    me = lax.axis_index(AXIS)
    half = lanes((v, LANES)) < m
    low_lane = lanes((v, LANES)) < r

    barrier = pltpu.get_barrier_semaphore()

    pairs = [
        (charges_h, cw.at[1]), (basis_h, basis), (leaf_transfer_h, leaf_transfer), (mid_transfer_h.at[0], mid_transfer),
        (mid_coupling_h, mid_coupling), (far_coupling_h, far_coupling), (box_coupling_h.at[0], box_coupling),
        (top_transfer_h, top_transfer),
    ]
    loads = [pltpu.make_async_copy(s, d, load_sem.at[i]) for i, (s, d) in enumerate(pairs)]
    width = near_blocks.shape[1] // CHUNKS

    def near_load(chunk):
        span = pl.ds(pl.multiple_of(chunk * width, width), width)
        return pltpu.make_async_copy(near_blocks_h.at[:, span], near_blocks.at[:, span], near_sem.at[chunk])

    for i in range(4):
        loads[i].start()
    for chunk in range(CHUNKS):
        near_load(chunk).start()
    for i in range(4, len(loads)):
        loads[i].start()
    tops = []
    for level in range(1, levels + 1):
        start = n - (n >> (level - 1))
        tops.append(pltpu.make_async_copy(
            top_coupling_h.at[start + (me >> level)], top_coupling.at[level - 1], top_sem.at[level - 1]))
    for copy in tops:
        copy.start()

    mesh_id = pl.DeviceIdType.MESH
    rounds = (n - 1).bit_length()
    odd_me = lax.rem(me, 2)
    outer = me - 1 + 2 * odd_me
    has_outer = (outer >= 0) & (outer < n)

    def partner(k):
        bit = lax.rem(me >> k, 2)
        return me + (1 << k) * (1 - 2 * bit)

    @pl.when(has_outer)
    def _():
        pl.semaphore_signal(barrier, inc=1, device_id=(outer,), device_id_type=mesh_id)

    for k in range(rounds):
        pl.semaphore_signal(barrier, inc=1, device_id=(partner(k),), device_id_type=mesh_id)

    loads[0].wait()
    loads[1].wait()
    span_points = child * m
    lane_leaf = lanes((v, span_points)) // m
    ups = []
    for c in range(groups):
        x = cw[1, :, c * span_points:(c + 1) * span_points].astype(F32)
        lhs = jnp.concatenate([jnp.where(lane_leaf == l, x, 0.0) for l in range(child)], axis=0).astype(BF16)
        b = basis[:, c * span_points:(c + 1) * span_points]
        up = diagonal(dot_nt(lhs, jnp.concatenate([b] * child, axis=0)), v, r0).astype(BF16)
        lw[1, :, c * child * r0:(c + 1) * child * r0] = up
        ups.append(up.astype(F32))
    loads[2].wait()
    loads[3].wait()
    quad = 4
    for g in range(groups // quad):
        lhs = jnp.concatenate(ups[g * quad:(g + 1) * quad], axis=0).astype(BF16)
        matrix = leaf_transfer[g * quad:(g + 1) * quad].reshape(quad * r, child * r0)
        mw[1, :, g * quad * r:(g + 1) * quad * r] = diagonal(dot_nt(lhs, matrix), v, r).astype(BF16)
    transfer = mid_transfer[...]
    box_up = dot_nt(mw[1], jnp.concatenate([transfer, transfer], axis=0))
    gathered[me] = box_up

    quad_mask = (rows((4 * r0, 4 * m)) // r0 == lanes((4 * r0, 4 * m)) // m).astype(F32).astype(BF16)
    for q in range(leaves // 4):
        b = basis[:, q * 4 * m:(q + 1) * 4 * m]
        masked_basis[q] = jnp.concatenate([b] * 4, axis=0) * quad_mask
    count = near_count[0]
    leaf_row = rows((leaves, LANES))
    slot_lane = lanes((leaves, LANES))
    assignment = []
    for b in range(capacity // LANES):
        hit = (leaf_row == near_target[b:b + 1, :]) & (slot_lane + b * LANES < count)
        assignment.append(jnp.where(hit, 1.0, 0.0).astype(BF16))
    per = len(assignment) // 4
    assignment = [jnp.concatenate(assignment[b * per:(b + 1) * per], axis=1) for b in range(4)]
    for b, value in enumerate(assignment):
        assigned[b] = value

    def spread_pairs(wide, tiles, per_box, box):
        x = wide[box].astype(F32)
        first = lax.rem(me + 3 + box, 4) * per_box
        for t in range(per_box // 2):
            tile = x[:, t * LANES:(t + 1) * LANES]
            turned = pltpu.roll(tile, LANES // 2, 1)
            tiles[first + 2 * t] = jnp.where(half, tile, turned)
            tiles[first + 2 * t + 1] = jnp.where(half, turned, tile)

    fold = LANES // r0
    lane_block = lanes((v, LANES)) // r0

    def spread_leaves(box):
        x = lw[box].astype(F32)
        first = lax.rem(me + 3 + box, 4) * leaves
        for t in range(leaves // fold):
            tile = x[:, t * LANES:(t + 1) * LANES]
            turned = [tile] + [pltpu.roll(tile, r0 * k, 1) for k in range(1, fold)]
            for p in range(fold):
                piece = turned[(0 - p) % fold]
                for w in range(1, fold):
                    piece = jnp.where(lane_block == w, turned[(w - p) % fold], piece)
                leaf_tiles[first + t * fold + p] = piece

    for tiles, per_box in ((charge_tiles, leaves), (leaf_tiles, leaves), (mid_tiles, groups)):
        unused = pl.ds(lax.rem(me + 2, 4) * per_box, per_box)
        tiles[unused] = jnp.zeros((per_box, v, LANES), F32)
    spread_pairs(cw, charge_tiles, leaves, 1)
    spread_leaves(1)
    spread_pairs(mw, mid_tiles, groups, 1)

    @pl.when(has_outer)
    def _():
        pl.semaphore_wait(barrier, rounds + 1)

    @pl.when(jnp.logical_not(has_outer))
    def _():
        pl.semaphore_wait(barrier, rounds)

    def exchange(k):
        group = pl.ds((me >> k) << k, 1 << k)
        return pltpu.make_async_remote_copy(
            src_ref=gathered.at[group], dst_ref=gathered.at[group], send_sem=all_send.at[k],
            recv_sem=all_recv.at[k], device_id=(partner(k),), device_id_type=mesh_id)

    sent = []

    def next_round():
        k = len(sent)
        if k > 0 and k <= rounds:
            sent[k - 1].wait_recv()
        if k < rounds:
            copy = exchange(k)
            copy.start()
            sent.append(copy)
        elif k == rounds:
            sent.append(None)

    wides = (cw, lw, mw)

    def halo(kind, side):
        wide = wides[kind]
        return pltpu.make_async_remote_copy(
            src_ref=wide.at[1], dst_ref=wide.at[2 - 2 * side], send_sem=halo_send.at[2 * kind + side],
            recv_sem=halo_recv.at[2 * kind + side], device_id=(me - 1 + 2 * side,),
            device_id_type=pl.DeviceIdType.MESH)

    def halo_starts(kind):
        @pl.when(me > 0)
        def _():
            halo(kind, 0).start()

        @pl.when(me < n - 1)
        def _():
            halo(kind, 1).start()

    def halo_arrive(kind):
        wide = wides[kind]

        @pl.when(me < n - 1)
        def _():
            halo(kind, 0).wait_recv()

        @pl.when(me > 0)
        def _():
            halo(kind, 1).wait_recv()

        @pl.when(me == 0)
        def _():
            wide[0] = jnp.zeros(wide.shape[1:], BF16)

        @pl.when(me == n - 1)
        def _():
            wide[2] = jnp.zeros(wide.shape[1:], BF16)

    def halo_sent(kind):
        @pl.when(me > 0)
        def _():
            halo(kind, 0).wait_send()

        @pl.when(me < n - 1)
        def _():
            halo(kind, 1).wait_send()

    next_round()
    halo_starts(1)
    halo_starts(0)
    halo_starts(2)

    halo_arrive(1)
    spread_leaves(0)
    spread_leaves(2)
    loads[5].wait()

    def far_step(c, carry):
        parts = []
        for l in range(child):
            tiles = []
            for t in range(k0 // fold):
                piece = leaf_tiles[far_source[t * fold, c * child + l] & (4 * leaves - 1)]
                for w in range(1, fold):
                    source = far_source[t * fold + w, c * child + l] & (4 * leaves - 1)
                    piece = jnp.where(lane_block == w, leaf_tiles[source], piece)
                tiles.append(piece)
            parts.append(jnp.concatenate(tiles, axis=1))
        lhs = jnp.concatenate(parts, axis=0).astype(BF16)
        matrix = far_coupling[c * child:(c + 1) * child].reshape(child * r0, k0 * r0)
        leaf_far[c] = diagonal(dot_nt(lhs, matrix), v, r0)
        return carry

    next_round()
    for c in range(groups):
        far_step(c, 0)
        if c % 4 == 3:
            next_round()

    halo_arrive(0)
    spread_pairs(cw, charge_tiles, leaves, 0)
    spread_pairs(cw, charge_tiles, leaves, 2)

    zero = jnp.zeros((2 * v, LANES), F32)
    wide_half = lanes((4 * v, LANES)) < m

    for chunk in range(CHUNKS):
        near_load(chunk).wait()
    parts = 4
    quarter = capacity // parts
    for g in range(quarter // 4):
        stacked = []
        matrices = []
        for h in range(parts):
            first = h * quarter + g * 4
            pieces = []
            for i in range(4):
                x = charge_tiles[near_source[first + i] & (4 * leaves - 1)]
                pieces.append(jnp.where(half, x, 0.0) if i % 2 == 0 else jnp.where(half, 0.0, x))
            upper = jnp.concatenate([pieces[0], pieces[1]], axis=0)
            lower = jnp.concatenate([pieces[2], pieces[3]], axis=0)
            stacked += [jnp.concatenate([upper, zero], axis=1), jnp.concatenate([zero, lower], axis=1)]
            matrices.append(near_blocks[:, first * m:(first + 4) * m])
        out = dot_nt(jnp.concatenate(stacked, axis=0).astype(BF16), jnp.concatenate(matrices, axis=0))
        q = 4 * v
        for w in range(2):
            a = out[2 * w * q:(2 * w + 1) * q, w * LANES:(w + 1) * LANES]
            b = out[(2 * w + 1) * q:(2 * w + 2) * q, w * LANES:(w + 1) * LANES]
            contribution[w, g * q:(g + 1) * q, :] = jnp.where(wide_half, a, b)
        if g in (quarter // 16, quarter // 8, 3 * quarter // 16):
            next_round()

    hits = assigned[...].reshape(parts * leaves, quarter)
    tall_half = lanes((leaves, LANES)) < m
    for u in range(v):
        c = jnp.concatenate(
            [contribution[w, pl.ds(u, quarter, stride=v), :] for w in range(2)], axis=1).astype(BF16)
        out = dot_nn(hits, c)
        total = jnp.zeros((leaves, LANES), F32)
        for w in range(2):
            a = out[2 * w * leaves:(2 * w + 1) * leaves, w * LANES:(w + 1) * LANES]
            b = out[(2 * w + 1) * leaves:(2 * w + 2) * leaves, w * LANES:(w + 1) * LANES]
            total = total + jnp.where(tall_half, a, b)
        near_rows[u * leaves:(u + 1) * leaves, :] = total + pltpu.roll(total, m, 1)

    halo_arrive(2)
    spread_pairs(mw, mid_tiles, groups, 0)
    spread_pairs(mw, mid_tiles, groups, 2)
    loads[4].wait()
    for g in range(groups // quad):
        parts = []
        for c in range(g * quad, (g + 1) * quad):
            tiles = []
            for t in range(k1 // 2):
                a = mid_tiles[mid_source[c, 2 * t] & (4 * groups - 1)]
                b = mid_tiles[mid_source[c, 2 * t + 1] & (4 * groups - 1)]
                tiles.append(jnp.where(half, a, b))
            parts.append(jnp.concatenate(tiles, axis=1))
        lhs = jnp.concatenate(parts, axis=0).astype(BF16)
        matrix = mid_coupling[g * quad:(g + 1) * quad].reshape(quad * r, k1 * r)
        mid_far[:, g * quad * r:(g + 1) * quad * r] = diagonal(dot_nt(lhs, matrix), v, r)

    loads[6].wait()
    loads[7].wait()
    for copy in tops:
        copy.wait()

    while len(sent) <= rounds:
        next_round()

    offset = 0
    for level in range(levels):
        size = n >> level
        start = n - size
        below = gathered if level == 0 else upward
        for q in range(size // 2):
            a = below[offset + 2 * q]
            b = below[offset + 2 * q + 1]
            t = top_transfer[start + q]
            upward[start + q] = exact_nt(jnp.where(low_lane, a, b), jnp.concatenate([t, t], axis=0))
        offset = start
    across = []
    for level in range(levels + 1):
        size = n >> level
        cluster = me >> level
        below = gathered if level == 0 else upward
        base = 0 if level == 0 else n - (n >> (level - 1))
        odd = lax.rem(cluster, 2)
        found = []
        for partner in (cluster - 2 - odd, cluster + 2 - 4 * odd, cluster + 3 - odd):
            inside = (partner >= 0) & (partner < size)
            safe = jnp.clip(partner, 0, size - 1)
            found.append(below[base + safe] * jnp.where(inside, 1.0, 0.0))
        g = box_coupling[...] if level == 0 else top_coupling[level - 1]
        g = jnp.concatenate([g, g], axis=0)
        across.append(exact_nt(jnp.where(low_lane, found[0], found[1]), g[:, :2 * r])
                      + exact_nt(found[2][:, :r], g[:, 2 * r:]))
    downward = across[levels]
    for level in range(levels - 1, -1, -1):
        cluster = me >> level
        start = n - (n >> level)
        pushed = exact_nn(downward[:, :r], top_transfer[start + (cluster >> 1)])
        turned = pltpu.roll(pushed, LANES // 2, 1)
        left = jnp.where(low_lane, pushed, turned)
        right = jnp.where(low_lane, turned, pushed)
        odd = lax.rem(cluster, 2).astype(F32)
        downward = across[level] + left * (1.0 - odd) + right * odd

    mid_push = dot_nn(downward[:, :r].astype(BF16), mid_transfer[...])
    mid_down = (mid_far[...] + mid_push).astype(BF16).astype(F32)
    near_half = lanes((v, LANES)) < m
    for pair in range(groups // 2):
        tile = mid_down[:, pair * LANES:(pair + 1) * LANES]
        lhs = jnp.concatenate([jnp.where(low_lane, tile, 0.0), jnp.where(low_lane, 0.0, tile)], axis=0).astype(BF16)
        matrix = leaf_transfer[2 * pair:2 * pair + 2].reshape(2 * r, child * r0)
        push = dot_nn(lhs, matrix)
        for s in range(2):
            c = 2 * pair + s
            leaf_down = (leaf_far[c] + push[s * v:(s + 1) * v]).astype(BF16)
            for h in range(child // 4):
                q = c * (child // 4) + h
                far = dot_nn(leaf_down[:, h * 4 * r0:(h + 1) * 4 * r0], masked_basis[q])
                for w in range(2):
                    leaf = q * 4 + 2 * w
                    a = near_rows[pl.ds(leaf, v, stride=leaves), :]
                    b = near_rows[pl.ds(leaf + 1, v, stride=leaves), :]
                    near = jnp.where(near_half, a, b)
                    out_ref[:, leaf * m:(leaf + 2) * m] = (far[:, w * LANES:(w + 1) * LANES] + near).astype(BF16)

    for copy in sent[:rounds]:
        copy.wait_send()
    for kind in range(3):
        halo_sent(kind)


def body(
    charges, leaf_basis, leaf_transfer, mid_transfer, far_source, far_coupling, mid_source, mid_coupling,
    box_coupling, top_transfer, top_coupling, near_target, near_source, near_count, near_blocks,
):
    n = lax.axis_size(AXIS)
    v, points = charges.shape
    leaves, k0 = far_source.shape
    m = points // leaves
    r0 = leaf_basis.shape[0]
    groups, k1 = mid_source.shape
    r = leaf_transfer.shape[1]
    capacity = near_target.shape[0]
    levels = (n // 4).bit_length() - 1
    sizes = (v, leaves, m, r0, groups, r, k0, k1, capacity)
    smem = pl.BlockSpec(memory_space=pltpu.SMEM)
    vmem = pl.BlockSpec(memory_space=pltpu.VMEM)
    hbm = pl.BlockSpec(memory_space=pl.ANY)
    dma = pltpu.SemaphoreType.DMA
    return pl.pallas_call(
        functools.partial(kernel, n, sizes),
        out_shape=jax.ShapeDtypeStruct(charges.shape, BF16),
        in_specs=[smem, smem, smem, smem, vmem] + [hbm] * 10,
        out_specs=vmem,
        scratch_shapes=[
            pltpu.VMEM((3, v, points), BF16),
            pltpu.VMEM((3, v, leaves * r0), BF16),
            pltpu.VMEM((3, v, groups * r), BF16),
            pltpu.VMEM((n, v, 2 * r), F32),
            pltpu.VMEM(leaf_basis.shape, BF16),
            pltpu.VMEM(leaf_transfer.shape, BF16),
            pltpu.VMEM(mid_transfer.shape[1:], BF16),
            pltpu.VMEM(far_coupling.shape, BF16),
            pltpu.VMEM(mid_coupling.shape, BF16),
            pltpu.VMEM(box_coupling.shape[1:], BF16),
            pltpu.VMEM(top_transfer.shape, BF16),
            pltpu.VMEM((levels,) + top_coupling.shape[1:], BF16),
            pltpu.VMEM(near_blocks.shape, BF16),
            pltpu.VMEM((4 * leaves, v, LANES), F32),
            pltpu.VMEM((4 * leaves, v, LANES), F32),
            pltpu.VMEM((4 * groups, v, LANES), F32),
            pltpu.VMEM((2, capacity // 4 * v, LANES), F32),
            pltpu.VMEM((v * leaves, 2 * m), F32),
            pltpu.VMEM((groups, v, leaves // groups * r0), F32),
            pltpu.VMEM((v, groups * r), F32),
            pltpu.VMEM((leaves // 4, 4 * r0, 4 * m), BF16),
            pltpu.VMEM((n, v, 2 * r), F32),
            pltpu.VMEM((4, leaves, capacity // 4), BF16),
            dma((8,)),
            dma((CHUNKS,)),
            dma((levels,)),
            dma((6,)),
            dma((6,)),
            dma(((n - 1).bit_length(),)),
            dma(((n - 1).bit_length(),)),
        ],
        compiler_params=pltpu.CompilerParams(
            collective_id=0, has_side_effects=True, vmem_limit_bytes=60 * 1024 * 1024),
    )(
        near_source, far_source.T, mid_source, near_count, near_target.reshape(capacity // LANES, LANES),
        charges, leaf_basis, leaf_transfer, mid_transfer, far_coupling, mid_coupling,
        box_coupling, top_transfer, top_coupling, near_blocks,
    )


def solution(mesh):
    c = "clusters"
    in_specs = (
        P(None, c), P(None, c), P(c, None, None), P(c, None, None), P(c, None), P(c, None, None),
        P(c, None), P(c, None, None), P(c, None, None), P(), P(), P(c), P(c), P(c), P(None, c),
    )
    return jax.shard_map(body, mesh=mesh, in_specs=in_specs, out_specs=P(None, c), check_vma=False)
```

```python
import functools

import jax
import jax.numpy as jnp
from jax import lax
from jax.experimental import pallas as pl
from jax.experimental.pallas import tpu as pltpu
from jax.sharding import PartitionSpec as P

F32 = jnp.float32
BF16 = jnp.bfloat16
AXIS = "clusters"
NT = (((1,), (1,)), ((), ()))
NN = (((1,), (0,)), ((), ()))
LANES = 128
CHUNKS = 8


def dot_nt(a, b):
    return lax.dot_general(a, b, NT, preferred_element_type=F32)


def dot_nn(a, b):
    return lax.dot_general(a, b, NN, preferred_element_type=F32)


def lanes(shape):
    return lax.broadcasted_iota(jnp.int32, shape, len(shape) - 1)


def rows(shape):
    return lax.broadcasted_iota(jnp.int32, shape, len(shape) - 2)


def split(x):
    high = x.astype(BF16).astype(F32)
    return jnp.concatenate([high, x - high], axis=0).astype(BF16)


def exact_nt(x, matrix):
    v = x.shape[0]
    out = dot_nt(split(x), matrix)
    return out[:v] + out[v:]


def exact_nn(x, matrix):
    v = x.shape[0]
    out = dot_nn(split(x), matrix)
    return out[:v] + out[v:]


def diagonal(out, v, width):
    blocks = out.shape[0] // v
    lane = lanes((v, out.shape[1])) // width
    total = jnp.zeros((v, out.shape[1]), F32)
    for block in range(blocks):
        total = jnp.where(lane == block, out[block * v:(block + 1) * v], total)
    return total


def kernel(
    n, sizes,
    near_source, far_source, mid_source, near_count, near_target,
    left_ref, right_ref, charges_h, basis_h, leaf_transfer_h, mid_transfer_h, far_coupling_h, mid_coupling_h,
    box_coupling_h, top_transfer_h, top_coupling_h, near_blocks_h,
    out_ref,
    cw, lw, mw, gathered, basis, leaf_transfer, mid_transfer, far_coupling, mid_coupling,
    box_coupling, top_transfer, top_coupling, near_blocks,
    charge_tiles, leaf_tiles, mid_tiles, contribution, near_rows, leaf_far, mid_far, masked_basis, upward, assigned,
    load_sem, near_sem, top_sem, halo_send, halo_recv, all_send, all_recv,
):
    v, leaves, m, r0, groups, r, k0, k1, capacity = sizes
    child = leaves // groups
    levels = (n // 4).bit_length() - 1
    me = lax.axis_index(AXIS)
    half = lanes((v, LANES)) < m
    low_lane = lanes((v, LANES)) < r

    barrier = pltpu.get_barrier_semaphore()

    pairs = [
        (charges_h, cw.at[1]), (basis_h, basis), (leaf_transfer_h, leaf_transfer), (mid_transfer_h.at[0], mid_transfer),
        (mid_coupling_h, mid_coupling), (far_coupling_h, far_coupling), (box_coupling_h.at[0], box_coupling),
        (top_transfer_h, top_transfer),
    ]
    loads = [pltpu.make_async_copy(s, d, load_sem.at[i]) for i, (s, d) in enumerate(pairs)]
    width = near_blocks.shape[1] // CHUNKS

    def near_load(chunk):
        span = pl.ds(pl.multiple_of(chunk * width, width), width)
        return pltpu.make_async_copy(near_blocks_h.at[:, span], near_blocks.at[:, span], near_sem.at[chunk])

    for i in range(4):
        loads[i].start()
    for chunk in range(CHUNKS):
        near_load(chunk).start()
    for i in range(4, len(loads)):
        loads[i].start()
    tops = []
    for level in range(1, levels + 1):
        start = n - (n >> (level - 1))
        tops.append(pltpu.make_async_copy(
            top_coupling_h.at[start + (me >> level)], top_coupling.at[level - 1], top_sem.at[level - 1]))
    for copy in tops:
        copy.start()

    def greet(step, carry):
        other = lax.rem(me + step, n)
        pl.semaphore_signal(barrier, inc=1, device_id=(other,), device_id_type=pl.DeviceIdType.MESH)
        return carry

    lax.fori_loop(1, n, greet, 0)

    loads[0].wait()
    loads[1].wait()
    span_points = child * m
    lane_leaf = lanes((v, span_points)) // m
    ups = []
    for c in range(groups):
        x = cw[1, :, c * span_points:(c + 1) * span_points].astype(F32)
        lhs = jnp.concatenate([jnp.where(lane_leaf == l, x, 0.0) for l in range(child)], axis=0).astype(BF16)
        b = basis[:, c * span_points:(c + 1) * span_points]
        up = diagonal(dot_nt(lhs, jnp.concatenate([b] * child, axis=0)), v, r0).astype(BF16)
        lw[1, :, c * child * r0:(c + 1) * child * r0] = up
        ups.append(up.astype(F32))
    loads[2].wait()
    loads[3].wait()
    quad = 4
    for g in range(groups // quad):
        lhs = jnp.concatenate(ups[g * quad:(g + 1) * quad], axis=0).astype(BF16)
        matrix = leaf_transfer[g * quad:(g + 1) * quad].reshape(quad * r, child * r0)
        mw[1, :, g * quad * r:(g + 1) * quad * r] = diagonal(dot_nt(lhs, matrix), v, r).astype(BF16)
    transfer = mid_transfer[...]
    box_up = dot_nt(mw[1], jnp.concatenate([transfer, transfer], axis=0))
    gathered[me] = box_up

    quad_mask = (rows((4 * r0, 4 * m)) // r0 == lanes((4 * r0, 4 * m)) // m).astype(F32).astype(BF16)
    for q in range(leaves // 4):
        b = basis[:, q * 4 * m:(q + 1) * 4 * m]
        masked_basis[q] = jnp.concatenate([b] * 4, axis=0) * quad_mask
    count = near_count[0]
    leaf_row = rows((leaves, LANES))
    slot_lane = lanes((leaves, LANES))
    assignment = []
    for b in range(capacity // LANES):
        hit = (leaf_row == near_target[b:b + 1, :]) & (slot_lane + b * LANES < count)
        assignment.append(jnp.where(hit, 1.0, 0.0).astype(BF16))
    per = len(assignment) // 4
    assignment = [jnp.concatenate(assignment[b * per:(b + 1) * per], axis=1) for b in range(4)]
    for b, value in enumerate(assignment):
        assigned[b] = value

    charge_boxes = (left_ref, cw.at[1], right_ref)
    mid_boxes = tuple(mw.at[box] for box in range(3))

    def spread_pairs(wide, tiles, per_box, box):
        x = wide[box][...].astype(F32)
        first = lax.rem(me + 3 + box, 4) * per_box
        for t in range(per_box // 2):
            tile = x[:, t * LANES:(t + 1) * LANES]
            turned = pltpu.roll(tile, LANES // 2, 1)
            tiles[first + 2 * t] = jnp.where(half, tile, turned)
            tiles[first + 2 * t + 1] = jnp.where(half, turned, tile)

    fold = LANES // r0
    lane_block = lanes((v, LANES)) // r0

    def spread_leaves(box):
        x = lw[box].astype(F32)
        first = lax.rem(me + 3 + box, 4) * leaves
        for t in range(leaves // fold):
            tile = x[:, t * LANES:(t + 1) * LANES]
            turned = [tile] + [pltpu.roll(tile, r0 * k, 1) for k in range(1, fold)]
            for p in range(fold):
                piece = turned[(0 - p) % fold]
                for w in range(1, fold):
                    piece = jnp.where(lane_block == w, turned[(w - p) % fold], piece)
                leaf_tiles[first + t * fold + p] = piece

    for tiles, per_box in ((charge_tiles, leaves), (leaf_tiles, leaves), (mid_tiles, groups)):
        unused = pl.ds(lax.rem(me + 2, 4) * per_box, per_box)
        tiles[unused] = jnp.zeros((per_box, v, LANES), F32)
    spread_pairs(charge_boxes, charge_tiles, leaves, 1)
    spread_leaves(1)
    spread_pairs(mid_boxes, mid_tiles, groups, 1)

    def everyone(step):
        other = lax.rem(me + step, n)
        return pltpu.make_async_remote_copy(
            src_ref=gathered.at[me], dst_ref=gathered.at[me], send_sem=all_send.at[step],
            recv_sem=all_recv.at[me], device_id=(other,), device_id_type=pl.DeviceIdType.MESH)

    def arrival(source):
        return pltpu.make_async_remote_copy(
            src_ref=gathered.at[source], dst_ref=gathered.at[source], send_sem=all_send.at[0],
            recv_sem=all_recv.at[source], device_id=(me,), device_id_type=pl.DeviceIdType.MESH)

    wides = (lw, mw)

    def halo(kind, side):
        wide = wides[kind]
        return pltpu.make_async_remote_copy(
            src_ref=wide.at[1], dst_ref=wide.at[2 - 2 * side], send_sem=halo_send.at[2 * kind + side],
            recv_sem=halo_recv.at[2 * kind + side], device_id=(me - 1 + 2 * side,),
            device_id_type=pl.DeviceIdType.MESH)

    def halo_starts(kind):
        @pl.when(me > 0)
        def _():
            halo(kind, 0).start()

        @pl.when(me < n - 1)
        def _():
            halo(kind, 1).start()

    def halo_arrive(kind):
        wide = wides[kind]

        @pl.when(me < n - 1)
        def _():
            halo(kind, 0).wait_recv()

        @pl.when(me > 0)
        def _():
            halo(kind, 1).wait_recv()

        @pl.when(me == 0)
        def _():
            wide[0] = jnp.zeros(wide.shape[1:], BF16)

        @pl.when(me == n - 1)
        def _():
            wide[2] = jnp.zeros(wide.shape[1:], BF16)

    def halo_sent(kind):
        @pl.when(me > 0)
        def _():
            halo(kind, 0).wait_send()

        @pl.when(me < n - 1)
        def _():
            halo(kind, 1).wait_send()

    def send_step(step, carry):
        everyone(step).start()
        return carry

    spread_pairs(charge_boxes, charge_tiles, leaves, 0)
    spread_pairs(charge_boxes, charge_tiles, leaves, 2)

    zero = jnp.zeros((2 * v, LANES), F32)
    wide_half = lanes((4 * v, LANES)) < m

    for chunk in range(CHUNKS):
        near_load(chunk).wait()
    parts = 4
    quarter = capacity // parts
    for g in range(quarter // 4):
        stacked = []
        matrices = []
        for h in range(parts):
            first = h * quarter + g * 4
            pieces = []
            for i in range(4):
                x = charge_tiles[near_source[first + i] & (4 * leaves - 1)]
                pieces.append(jnp.where(half, x, 0.0) if i % 2 == 0 else jnp.where(half, 0.0, x))
            upper = jnp.concatenate([pieces[0], pieces[1]], axis=0)
            lower = jnp.concatenate([pieces[2], pieces[3]], axis=0)
            stacked += [jnp.concatenate([upper, zero], axis=1), jnp.concatenate([zero, lower], axis=1)]
            matrices.append(near_blocks[:, first * m:(first + 4) * m])
        out = dot_nt(jnp.concatenate(stacked, axis=0).astype(BF16), jnp.concatenate(matrices, axis=0))
        q = 4 * v
        for w in range(2):
            a = out[2 * w * q:(2 * w + 1) * q, w * LANES:(w + 1) * LANES]
            b = out[(2 * w + 1) * q:(2 * w + 2) * q, w * LANES:(w + 1) * LANES]
            contribution[w, g * q:(g + 1) * q, :] = jnp.where(wide_half, a, b)
        if g == quarter // 8:
            pl.semaphore_wait(barrier, n - 1)
            halo_starts(0)
            halo_starts(1)
            lax.fori_loop(1, n, send_step, 0)

    hits = assigned[...].reshape(parts * leaves, quarter)
    tall_half = lanes((leaves, LANES)) < m
    for u in range(v):
        c = jnp.concatenate(
            [contribution[w, pl.ds(u, quarter, stride=v), :] for w in range(2)], axis=1).astype(BF16)
        out = dot_nn(hits, c)
        total = jnp.zeros((leaves, LANES), F32)
        for w in range(2):
            a = out[2 * w * leaves:(2 * w + 1) * leaves, w * LANES:(w + 1) * LANES]
            b = out[(2 * w + 1) * leaves:(2 * w + 2) * leaves, w * LANES:(w + 1) * LANES]
            total = total + jnp.where(tall_half, a, b)
        near_rows[u * leaves:(u + 1) * leaves, :] = total + pltpu.roll(total, m, 1)

    halo_arrive(0)
    spread_leaves(0)
    spread_leaves(2)
    loads[5].wait()

    def far_step(c, carry):
        parts = []
        for l in range(child):
            tiles = []
            for t in range(k0 // fold):
                piece = leaf_tiles[far_source[t * fold, c * child + l] & (4 * leaves - 1)]
                for w in range(1, fold):
                    source = far_source[t * fold + w, c * child + l] & (4 * leaves - 1)
                    piece = jnp.where(lane_block == w, leaf_tiles[source], piece)
                tiles.append(piece)
            parts.append(jnp.concatenate(tiles, axis=1))
        lhs = jnp.concatenate(parts, axis=0).astype(BF16)
        matrix = far_coupling[c * child:(c + 1) * child].reshape(child * r0, k0 * r0)
        leaf_far[c] = diagonal(dot_nt(lhs, matrix), v, r0)
        return carry

    for c in range(groups):
        far_step(c, 0)

    halo_arrive(1)
    spread_pairs(mid_boxes, mid_tiles, groups, 0)
    spread_pairs(mid_boxes, mid_tiles, groups, 2)
    loads[4].wait()
    for g in range(groups // quad):
        parts = []
        for c in range(g * quad, (g + 1) * quad):
            tiles = []
            for t in range(k1 // 2):
                a = mid_tiles[mid_source[c, 2 * t] & (4 * groups - 1)]
                b = mid_tiles[mid_source[c, 2 * t + 1] & (4 * groups - 1)]
                tiles.append(jnp.where(half, a, b))
            parts.append(jnp.concatenate(tiles, axis=1))
        lhs = jnp.concatenate(parts, axis=0).astype(BF16)
        matrix = mid_coupling[g * quad:(g + 1) * quad].reshape(quad * r, k1 * r)
        mid_far[:, g * quad * r:(g + 1) * quad * r] = diagonal(dot_nt(lhs, matrix), v, r)

    loads[6].wait()
    loads[7].wait()
    for copy in tops:
        copy.wait()

    def arrive_step(step, carry):
        arrival(lax.rem(me + step, n)).wait_recv()
        return carry

    lax.fori_loop(1, n, arrive_step, 0)

    offset = 0
    for level in range(levels):
        size = n >> level
        start = n - size
        below = gathered if level == 0 else upward
        for q in range(size // 2):
            a = below[offset + 2 * q]
            b = below[offset + 2 * q + 1]
            t = top_transfer[start + q]
            upward[start + q] = exact_nt(jnp.where(low_lane, a, b), jnp.concatenate([t, t], axis=0))
        offset = start
    across = []
    for level in range(levels + 1):
        size = n >> level
        cluster = me >> level
        below = gathered if level == 0 else upward
        base = 0 if level == 0 else n - (n >> (level - 1))
        odd = lax.rem(cluster, 2)
        found = []
        for partner in (cluster - 2 - odd, cluster + 2 - 4 * odd, cluster + 3 - odd):
            inside = (partner >= 0) & (partner < size)
            safe = jnp.clip(partner, 0, size - 1)
            found.append(below[base + safe] * jnp.where(inside, 1.0, 0.0))
        g = box_coupling[...] if level == 0 else top_coupling[level - 1]
        g = jnp.concatenate([g, g], axis=0)
        across.append(exact_nt(jnp.where(low_lane, found[0], found[1]), g[:, :2 * r])
                      + exact_nt(found[2][:, :r], g[:, 2 * r:]))
    downward = across[levels]
    for level in range(levels - 1, -1, -1):
        cluster = me >> level
        start = n - (n >> level)
        pushed = exact_nn(downward[:, :r], top_transfer[start + (cluster >> 1)])
        turned = pltpu.roll(pushed, LANES // 2, 1)
        left = jnp.where(low_lane, pushed, turned)
        right = jnp.where(low_lane, turned, pushed)
        odd = lax.rem(cluster, 2).astype(F32)
        downward = across[level] + left * (1.0 - odd) + right * odd

    mid_push = dot_nn(downward[:, :r].astype(BF16), mid_transfer[...])
    mid_down = (mid_far[...] + mid_push).astype(BF16).astype(F32)
    near_half = lanes((v, LANES)) < m
    for pair in range(groups // 2):
        tile = mid_down[:, pair * LANES:(pair + 1) * LANES]
        lhs = jnp.concatenate([jnp.where(low_lane, tile, 0.0), jnp.where(low_lane, 0.0, tile)], axis=0).astype(BF16)
        matrix = leaf_transfer[2 * pair:2 * pair + 2].reshape(2 * r, child * r0)
        push = dot_nn(lhs, matrix)
        for s in range(2):
            c = 2 * pair + s
            leaf_down = (leaf_far[c] + push[s * v:(s + 1) * v]).astype(BF16)
            for h in range(child // 4):
                q = c * (child // 4) + h
                far = dot_nn(leaf_down[:, h * 4 * r0:(h + 1) * 4 * r0], masked_basis[q])
                for w in range(2):
                    leaf = q * 4 + 2 * w
                    a = near_rows[pl.ds(leaf, v, stride=leaves), :]
                    b = near_rows[pl.ds(leaf + 1, v, stride=leaves), :]
                    near = jnp.where(near_half, a, b)
                    out_ref[:, leaf * m:(leaf + 2) * m] = (far[:, w * LANES:(w + 1) * LANES] + near).astype(BF16)

    def sent_step(step, carry):
        everyone(step).wait_send()
        return carry

    lax.fori_loop(1, n, sent_step, 0)
    for kind in range(2):
        halo_sent(kind)


def body(
    charges, leaf_basis, leaf_transfer, mid_transfer, far_source, far_coupling, mid_source, mid_coupling,
    box_coupling, top_transfer, top_coupling, near_target, near_source, near_count, near_blocks,
):
    n = lax.axis_size(AXIS)
    v, points = charges.shape
    leaves, k0 = far_source.shape
    m = points // leaves
    r0 = leaf_basis.shape[0]
    groups, k1 = mid_source.shape
    r = leaf_transfer.shape[1]
    capacity = near_target.shape[0]
    levels = (n // 4).bit_length() - 1
    left = lax.ppermute(charges, AXIS, [(i, i + 1) for i in range(n - 1)])
    right = lax.ppermute(charges, AXIS, [(i + 1, i) for i in range(n - 1)])
    sizes = (v, leaves, m, r0, groups, r, k0, k1, capacity)
    smem = pl.BlockSpec(memory_space=pltpu.SMEM)
    vmem = pl.BlockSpec(memory_space=pltpu.VMEM)
    hbm = pl.BlockSpec(memory_space=pl.ANY)
    dma = pltpu.SemaphoreType.DMA
    return pl.pallas_call(
        functools.partial(kernel, n, sizes),
        out_shape=jax.ShapeDtypeStruct(charges.shape, BF16),
        in_specs=[smem, smem, smem, smem, vmem, vmem, vmem] + [hbm] * 10,
        out_specs=vmem,
        scratch_shapes=[
            pltpu.VMEM((3, v, points), BF16),
            pltpu.VMEM((3, v, leaves * r0), BF16),
            pltpu.VMEM((3, v, groups * r), BF16),
            pltpu.VMEM((n, v, 2 * r), F32),
            pltpu.VMEM(leaf_basis.shape, BF16),
            pltpu.VMEM(leaf_transfer.shape, BF16),
            pltpu.VMEM(mid_transfer.shape[1:], BF16),
            pltpu.VMEM(far_coupling.shape, BF16),
            pltpu.VMEM(mid_coupling.shape, BF16),
            pltpu.VMEM(box_coupling.shape[1:], BF16),
            pltpu.VMEM(top_transfer.shape, BF16),
            pltpu.VMEM((levels,) + top_coupling.shape[1:], BF16),
            pltpu.VMEM(near_blocks.shape, BF16),
            pltpu.VMEM((4 * leaves, v, LANES), F32),
            pltpu.VMEM((4 * leaves, v, LANES), F32),
            pltpu.VMEM((4 * groups, v, LANES), F32),
            pltpu.VMEM((2, capacity // 4 * v, LANES), F32),
            pltpu.VMEM((v * leaves, 2 * m), F32),
            pltpu.VMEM((groups, v, leaves // groups * r0), F32),
            pltpu.VMEM((v, groups * r), F32),
            pltpu.VMEM((leaves // 4, 4 * r0, 4 * m), BF16),
            pltpu.VMEM((n, v, 2 * r), F32),
            pltpu.VMEM((4, leaves, capacity // 4), BF16),
            dma((10,)),
            dma((CHUNKS,)),
            dma((levels,)),
            dma((4,)),
            dma((4,)),
            dma((n,)),
            dma((n,)),
        ],
        compiler_params=pltpu.CompilerParams(
            collective_id=0, has_side_effects=True, vmem_limit_bytes=60 * 1024 * 1024),
    )(
        near_source, far_source.T, mid_source, near_count, near_target.reshape(capacity // LANES, LANES),
        left, right, charges, leaf_basis, leaf_transfer, mid_transfer, far_coupling, mid_coupling,
        box_coupling, top_transfer, top_coupling, near_blocks,
    )


def solution(mesh):
    c = "clusters"
    in_specs = (
        P(None, c), P(None, c), P(c, None, None), P(c, None, None), P(c, None), P(c, None, None),
        P(c, None), P(c, None, None), P(c, None, None), P(), P(), P(c), P(c), P(c), P(None, c),
    )
    return jax.shard_map(body, mesh=mesh, in_specs=in_specs, out_specs=P(None, c), check_vma=False)
```
